32 devices in a mesh: member: 2 (over y), lat: 16 (over z, x, core).
Axes of the slice: x: 2, y: 2, z: 4, core: 2. Of those that a mesh axis runs over, the one named last changes fastest.
Arguments:
- increment: float32 [274, 256, 128], P('member', 'lat'), parts along dimension 0, may hold values from -6 to 6
- filter_taps: int32 [4, 2, 2, 5], replicated, may hold values from 1 to 8
- band_roots: float32 [5, 137, 137], replicated, may hold values from -1 to 1
Outputs:
- adjoint: float32 [274, 256, 128], P('member', 'lat'), parts along dimension 0
The draws below stay inside these ranges and needn't reach their ends.
There are 2 independent parts, one for each index of `member`. The reference program is written for one: setup_inputs(seed, part) draws one part's arguments, and reference() takes and returns one part's arrays. A program takes and returns all parts, laid end to end along the dimension named above; an argument that names none is the same for every part. Nothing has to cross between parts.
All inputs are finite; a program needn't handle non-finite values.
Results may differ from the reference program's by a relative error of at most 0.0001.
Values sent between devices are 32-bit elements; how exact they have to be, the bound alone decides.
A program may use at most 64 MiB of HBM per device.

```python
import math
import jax
import jax.numpy as jnp
from jax import lax

LEV = 137
NLON = 128
LEVELS = 4
BANDS = 5
NLAT = 256


def with_ends(values, rng, least, top_value):
    index_at = [jax.random.randint(jax.random.fold_in(rng, axis), (), 0, length) for axis, length in enumerate(values.shape)]
    main_axis = values.shape.index(max(values.shape))
    next_to = index_at[:main_axis] + [(index_at[main_axis] + 1) % values.shape[main_axis]] + index_at[main_axis + 1:]
    return values.at[tuple(index_at)].set(least).at[tuple(next_to)].set(top_value)


def levels(key, extent, split, least, high):
    gain = 1.0
    for dim, blocks in split:
        heights = jax.random.uniform(jax.random.fold_in(jax.random.fold_in(key, 6), dim), (blocks,), jnp.float32, least / len(split), high / len(split))
        gain = gain * jnp.repeat(jnp.exp(heights), extent[dim] // blocks).reshape((-1,) + (1,) * (len(extent) - 1 - dim))
    return gain


def normal_values(key, extent, scale, reach, pieces=(), held_as=jnp.bfloat16):
    values = scale * jax.random.normal(key, extent, jnp.float32)
    if pieces:
        values = values * levels(key, extent, pieces, -0.22, 0.18)
    return jnp.clip(values, -reach, reach).astype(held_as)


def setup_inputs(seed: int = 0, part: int = 0) -> dict:
    arg_keys = jax.random.split(jax.random.key(seed), 4)
    part_keys = jax.random.split(jax.random.fold_in(arg_keys[3], part), 4)
    increment = normal_values(part_keys[0], (LEV, NLAT, NLON), 1.0, 6.0, ((1, 16),), jnp.float32)
    filter_taps = with_ends(jax.random.randint(arg_keys[1], (LEVELS, 2, 2, 5), 1, 9), jax.random.fold_in(arg_keys[1], 1), 1, 8).astype(jnp.int32)
    band_roots = normal_values(arg_keys[2], (BANDS, LEV, LEV), 0.17, 1.0, (), jnp.float32)
    return {"increment": increment, "filter_taps": filter_taps, "band_roots": band_roots}


ROOT_TWO = math.sqrt(2.0)

def make_filters(filter_taps):
    coeffs = filter_taps.astype(jnp.float32)
    sign_pattern = jnp.array([1.0, -1.0, 1.0, -1.0, 1.0], dtype=jnp.float32)
    lowpass = ROOT_TWO * coeffs[:, :, 0] / lax.optimization_barrier(jnp.sum(coeffs[:, :, 0], axis=-1, keepdims=True))
    highpass = sign_pattern * coeffs[:, :, 1] / jnp.sqrt(lax.optimization_barrier(jnp.sum(coeffs[:, :, 1] * coeffs[:, :, 1], axis=-1, keepdims=True)))
    return jnp.stack([lowpass, highpass], axis=2)

def filter_down(padded, coeffs, length, along):
    summed = coeffs[0] * lax.slice_in_dim(padded, 0, length, 2, along)
    for offset in range(1, 5):
        summed = summed + coeffs[offset] * lax.slice_in_dim(padded, offset, offset + length, 2, along)
    return summed

def filter_up(padded, coeffs, length, along):
    summed = coeffs[0] * lax.slice_in_dim(padded, 4, 4 + length, 1, along)
    for offset in range(1, 5):
        summed = summed + coeffs[offset] * lax.slice_in_dim(padded, 4 - offset, 4 - offset + length, 1, along)
    return summed

def spread_zeros(values, along):
    stacked = jnp.stack([values, jnp.zeros_like(values)], axis=along + 1)
    new_shape = values.shape[:along] + (2 * values.shape[along],) + values.shape[along + 1:]
    return stacked.reshape(new_shape)

def pad_cols(values):
    padding = [(0, 0)] * (values.ndim - 1) + [(2, 2)]
    return jnp.pad(values, padding)

def analyze(values, level_filters, row_rim):
    row_count = values.shape[1]
    col_count = values.shape[2]
    padded = row_rim(values[None], 2)[0]
    halves = jnp.stack([filter_down(padded, level_filters[0, 0], row_count, 1), filter_down(padded, level_filters[0, 1], row_count, 1)])
    widened = pad_cols(halves)
    low_parts = filter_down(widened, level_filters[1, 0], col_count, 3)
    high_parts = filter_down(widened, level_filters[1, 1], col_count, 3)
    return (low_parts[0], jnp.stack([high_parts[0], low_parts[1], high_parts[1]]))

def synthesize(coarse, details, level_filters, row_rim):
    row_count = 2 * coarse.shape[1]
    col_count = 2 * coarse.shape[2]
    low_parts = pad_cols(spread_zeros(jnp.stack([coarse, details[1]]), 3))
    high_parts = pad_cols(spread_zeros(jnp.stack([details[0], details[2]]), 3))
    halves = filter_up(low_parts, level_filters[1, 0], col_count, 3) + filter_up(high_parts, level_filters[1, 1], col_count, 3)
    padded = spread_zeros(row_rim(halves, 1), 2)
    return filter_up(padded[0], level_filters[0, 0], row_count, 1) + filter_up(padded[1], level_filters[0, 1], row_count, 1)

def vertical(matrix, band, transposed):
    chosen = matrix.T if transposed else matrix
    return jnp.einsum('ij,...jrc->...irc', chosen, band, precision=lax.Precision.HIGHEST, preferred_element_type=jnp.float32)

def zero_rim(values, rim_width):
    padding = [(0, 0)] * values.ndim
    padding[2] = (rim_width, rim_width)
    return jnp.pad(values, padding)

def transform(values, level_filters, band_roots, transposed):
    band_list = []
    coarse = values
    for level_index in range(LEVELS):
        coarse, details = analyze(coarse, level_filters[level_index], zero_rim)
        band_list.append(vertical(band_roots[level_index], details, transposed))
    coarse = vertical(band_roots[LEVELS], coarse, transposed)
    for level_index in reversed(range(LEVELS)):
        coarse = synthesize(coarse, band_list[level_index], level_filters[level_index], zero_rim)
    return coarse

def reference(increment, filter_taps, band_roots):
    level_filters = make_filters(filter_taps)
    shaped = transform(increment, level_filters, band_roots, False)
    return transform(shaped, level_filters, band_roots, True)
```

```python
import functools
import math

import jax
import jax.numpy as jnp
from jax import lax
from jax.experimental import pallas as pl
from jax.experimental.pallas import tpu as pltpu
from jax.sharding import PartitionSpec as P

LEVELS = 4
ROOT_TWO = math.sqrt(2.0)
F32, BF16 = jnp.float32, jnp.bfloat16


def make_filters(filter_taps):
    coeffs = filter_taps.astype(F32)
    signs = jnp.array([1.0, -1.0, 1.0, -1.0, 1.0], dtype=F32)
    lowpass = ROOT_TWO * coeffs[:, :, 0] / jnp.sum(coeffs[:, :, 0], axis=-1, keepdims=True)
    highpass = (
        signs
        * coeffs[:, :, 1]
        / jnp.sqrt(jnp.sum(coeffs[:, :, 1] * coeffs[:, :, 1], axis=-1, keepdims=True))
    )
    return jnp.stack([lowpass, highpass], axis=2)


def halves_of(x):
    high = x.astype(BF16)
    return high, (x - high.astype(F32)).astype(BF16)


def dot(a, b):
    return jnp.dot(a, b, preferred_element_type=F32)


def kernel(lats, taps, x_hbm, roots, out, *scratch):
    xs = (scratch[0:4], (scratch[4],) + scratch[5:8])
    tops, hs, lvs = scratch[8], scratch[9:13], scratch[13:17]
    gs = (scratch[17:21], scratch[21:25])
    ks = (scratch[25:29], scratch[29:33])
    wmats, mats, sends, recvs, load_sem = scratch[33:]
    tile, lev, lanes = x_hbm.shape
    me = lax.axis_index("lat")
    has_down, has_up = me > 0, me < lats - 1
    slots = iter(range(10_000))

    def tap(level, direction, kind, k):
        return taps[((level * 2 + direction) * 2 + kind) * 5 + k]

    def exchange(src_up, dst_up, src_down, dst_down):
        up_slot, down_slot = next(slots), next(slots)
        up = pltpu.make_async_remote_copy(
            src_ref=src_up, dst_ref=dst_up, send_sem=sends.at[up_slot],
            recv_sem=recvs.at[up_slot], device_id={"lat": jnp.minimum(me + 1, lats - 1)},
            device_id_type=pl.DeviceIdType.MESH,
        )
        down = pltpu.make_async_remote_copy(
            src_ref=src_down, dst_ref=dst_down, send_sem=sends.at[down_slot],
            recv_sem=recvs.at[down_slot], device_id={"lat": jnp.maximum(me - 1, 0)},
            device_id_type=pl.DeviceIdType.MESH,
        )

        @pl.when(has_up)
        def _():
            up.start()

        @pl.when(has_down)
        def _():
            down.start()

        def arrive():
            @pl.when(has_down)
            def _():
                up.wait_recv()

            @pl.when(has_up)
            def _():
                down.wait_recv()

        def sent():
            @pl.when(has_up)
            def _():
                up.wait_send()

            @pl.when(has_down)
            def _():
                down.wait_send()

        pending.append(sent)
        return arrive

    pending = []
    load = pltpu.make_async_copy(x_hbm, xs[0][0].at[pl.ds(2, tile)], load_sem)
    load.start()

    barrier = pltpu.get_barrier_semaphore()

    @pl.when(has_down)
    def _():
        pl.semaphore_signal(
            barrier, inc=1, device_id={"lat": jnp.maximum(me - 1, 0)},
            device_id_type=pl.DeviceIdType.MESH,
        )

    @pl.when(has_up)
    def _():
        pl.semaphore_signal(
            barrier, inc=1, device_id={"lat": jnp.minimum(me + 1, lats - 1)},
            device_id_type=pl.DeviceIdType.MESH,
        )

    pl.semaphore_wait(barrier, has_down.astype(jnp.int32) + has_up.astype(jnp.int32))

    arrive = exchange(
        x_hbm.at[pl.ds(tile - 2, 2)], xs[0][0].at[pl.ds(0, 2)],
        x_hbm.at[pl.ds(0, 1)], xs[0][0].at[pl.ds(tile + 2, 1)],
    )

    def zeros(ref, start, count):
        for r in range(count):
            ref[start + r] = jnp.zeros(ref.shape[1:], F32)

    rims = []
    for t in range(2):
        for j in range(LEVELS):
            n = tile >> (j + 1)
            if not (t == 1 and j == 0):
                rims.append((xs[t][j], 2, 1, 2 * n + 2))
            rim = 2 if t == 0 and j == 0 else 1
            rims.append((gs[t][j], rim, rim, n + rim))
            rims.append((ks[t][j], rim, rim, n + rim))

    @pl.when(jnp.logical_not(has_down))
    def _():
        for ref, below, _, _ in rims:
            zeros(ref, 0, below)

    @pl.when(jnp.logical_not(has_up))
    def _():
        for ref, _, above, at in rims:
            zeros(ref, at, above)

    for j in range(LEVELS):
        width = lanes >> j
        for flip in range(2):
            c = lax.broadcasted_iota(jnp.int32, (lanes, lanes), flip)
            o = lax.broadcasted_iota(jnp.int32, (lanes, lanes), 1 - flip)
            is_low = o < width // 2
            t = c - 2 * jnp.where(is_low, o, o - width // 2) + 2
            w = jnp.zeros((lanes, lanes), F32)
            for k in range(5):
                w = jnp.where(t == k, jnp.where(is_low, tap(j, 1, 0, k), tap(j, 1, 1, k)), w)
            w = jnp.where((c < width) & (o < width), w, 0.0)
            high, low = halves_of(w)
            at = 2 * j + flip
            wmats[at, pl.ds(0, lanes), pl.ds(0, lanes)] = high
            wmats[at, pl.ds(0, lanes), pl.ds(lanes, lanes)] = low
            wmats[at, pl.ds(lanes, lanes), pl.ds(0, lanes)] = high
            wmats[at, pl.ds(lanes, lanes), pl.ds(lanes, lanes)] = jnp.zeros_like(low)
    for b in range(roots.shape[0]):
        high, low = halves_of(roots[b])
        mats[b, pl.ds(0, lev)] = high
        mats[b, pl.ds(lev, lev)] = low

    def along_lon(x, at):
        high, low = halves_of(x)
        r = dot(jnp.concatenate([high, low], axis=1), wmats[at])
        return r[:, :lanes] + r[:, lanes:]

    def vertical(x, t, band):
        b = t * (LEVELS + 1) + band
        high, low = halves_of(x)
        r = dot(mats[b], high)
        return r[:lev] + r[lev:] + dot(mats[b, pl.ds(0, lev)], low)

    def loop(start, stop, body):
        if stop - start == 1:
            body(start)
        elif stop > start:
            lax.fori_loop(start, stop, lambda i, _: (body(i), 0)[1], 0)

    lane = lax.broadcasted_iota(jnp.int32, (lev, lanes), 1)

    def transform(t, arrive):
        k_arrivals = [None] * LEVELS
        for j in range(LEVELS):
            n = tile >> (j + 1)
            x = xs[t][j]
            following = xs[t][j + 1] if j + 1 < LEVELS else tops
            lead = 2 if j + 1 < LEVELS else 0

            def analyse(i):
                rows = [x[2 * i + k] for k in range(5)]
                low = sum(tap(j, 0, 0, k) * rows[k] for k in range(5))
                high = sum(tap(j, 0, 1, k) * rows[k] for k in range(5))
                both = along_lon(jnp.concatenate([low, high], axis=0), 2 * j)
                following[i + lead] = both[:lev]
                hs[j][i] = both[lev:]

            loop(1, n - 1, analyse)
            if arrive is not None:
                arrive()
            analyse(0)
            if n > 1:
                analyse(n - 1)
            arrive = None
            if j + 1 < LEVELS:
                arrive = exchange(
                    following.at[pl.ds(n, 2)], following.at[pl.ds(0, 2)],
                    following.at[pl.ds(2, 1)], following.at[pl.ds(n + 2, 1)],
                )
            rim = 2 if t == 0 and j == 0 else 1
            k_ref = ks[t][j]

            def weigh(i):
                pair = jnp.concatenate([following[i + lead], hs[j][i]], axis=1)
                pair = vertical(pair, t, j)
                lvs[j][i] = pair[:, :lanes]
                k_ref[i + rim] = along_lon(pair[:, lanes:], 2 * j + 1)

            loop(0, n, weigh)
            k_arrivals[j] = exchange(
                k_ref.at[pl.ds(n, rim)], k_ref.at[pl.ds(0, rim)],
                k_ref.at[pl.ds(rim, rim)], k_ref.at[pl.ds(n + rim, rim)],
            )
        for j in reversed(range(LEVELS)):
            n = tile >> (j + 1)
            rim = 2 if t == 0 and j == 0 else 1
            g_ref, k_ref = gs[t][j], ks[t][j]

            def lift(i, coarse):
                chosen = jnp.where(lane < (lanes >> (j + 1)), coarse, lvs[j][i])
                g_ref[i + rim] = along_lon(chosen, 2 * j + 1)

            if j == LEVELS - 1:
                lift(0, vertical(tops[0], t, LEVELS))
            else:
                def both(m, lift=lift, make=make):
                    even, odd = make(m)
                    lift(2 * m, even)
                    lift(2 * m + 1, odd)

                loop(0, n // 2, both)
            g_arrive = exchange(
                g_ref.at[pl.ds(n, rim)], g_ref.at[pl.ds(0, rim)],
                g_ref.at[pl.ds(rim, rim)], g_ref.at[pl.ds(n + rim, rim)],
            )
            k_arrivals[j]()
            g_arrive()

            def make(m, j=j, rim=rim, g_ref=g_ref, k_ref=k_ref, even_only=False):
                g = [g_ref[m + rim + s] for s in ((-1, 0, 1))]
                k = [k_ref[m + rim + s] for s in ((-1, 0, 1))]
                even = sum(tap(j, 0, 0, 4 - 2 * s) * g[s] + tap(j, 0, 1, 4 - 2 * s) * k[s] for s in range(3))
                if even_only:
                    return even
                odd = (
                    tap(j, 0, 0, 3) * g[1] + tap(j, 0, 0, 1) * g[2]
                    + tap(j, 0, 1, 3) * k[1] + tap(j, 0, 1, 1) * k[2]
                )
                return even, odd

        return make

    load.wait()
    make = transform(0, arrive)
    shaped = xs[1][0]

    def keep(m):
        shaped[2 * m + 2], shaped[2 * m + 3] = make(m)

    loop(0, tile // 2, keep)
    even, odd = make(-1)
    inside = jnp.where(has_down, 1.0, 0.0).astype(F32)
    shaped[0], shaped[1] = inside * even, inside * odd
    shaped[tile + 2] = jnp.where(has_up, 1.0, 0.0).astype(F32) * make(tile // 2, even_only=True)

    make = transform(1, None)

    def put(m):
        out[2 * m], out[2 * m + 1] = make(m)

    loop(0, tile // 2, put)
    for sent in pending:
        sent()


def on_device(increment, filter_taps, band_roots, lats):
    lev, tile, lanes = increment.shape
    padded = -(-lev // 16) * 16
    taps = make_filters(filter_taps).reshape(-1)
    x = jnp.pad(jnp.transpose(increment, (1, 0, 2)), ((0, 0), (0, padded - lev), (0, 0)))
    roots = jnp.pad(band_roots, ((0, 0), (0, padded - lev), (0, padded - lev)))
    roots = jnp.concatenate([roots, jnp.swapaxes(roots, 1, 2)])

    def slabs(count):
        return pltpu.VMEM((count, padded, lanes), F32)

    counts = [tile >> (j + 1) for j in range(LEVELS)]
    scratch = [slabs(2 * n + 3) for n in counts] * 2
    scratch += [slabs(1)] + [slabs(n) for n in counts] * 2
    for _ in range(2):
        scratch += [slabs(n + (4 if j == 0 else 2)) for j, n in enumerate(counts)]
        scratch += [slabs(n + 2) for n in counts]
    copies = 2 * (LEVELS + 2 * LEVELS) * 2 - 2
    scratch += [
        pltpu.VMEM((2 * LEVELS, 2 * lanes, 2 * lanes), BF16),
        pltpu.VMEM((2 * (LEVELS + 1), 2 * padded, padded), BF16),
        pltpu.SemaphoreType.DMA((copies,)),
        pltpu.SemaphoreType.DMA((copies,)),
        pltpu.SemaphoreType.DMA,
    ]
    y = pl.pallas_call(
        functools.partial(kernel, lats),
        out_shape=jax.ShapeDtypeStruct((tile, padded, lanes), F32),
        in_specs=[
            pl.BlockSpec(memory_space=pltpu.SMEM),
            pl.BlockSpec(memory_space=pl.ANY),
            pl.BlockSpec(memory_space=pltpu.VMEM),
        ],
        out_specs=pl.BlockSpec(memory_space=pltpu.VMEM),
        scratch_shapes=scratch,
        compiler_params=pltpu.CompilerParams(
            collective_id=0, has_side_effects=True, vmem_limit_bytes=48 << 20
        ),
    )(taps, x, roots)
    return jnp.transpose(y[:, :lev], (1, 0, 2))


def solution(mesh):
    placed = (P("member", "lat", None), P(), P())
    return jax.shard_map(
        functools.partial(on_device, lats=mesh.shape["lat"]),
        mesh=mesh, in_specs=placed, out_specs=P("member", "lat", None), check_vma=False,
    )
```

```python
import functools
import math

import jax
import jax.numpy as jnp
from jax import lax
from jax.experimental import pallas as pl
from jax.experimental.pallas import tpu as pltpu
from jax.sharding import PartitionSpec as P

LEVELS = 4
ROOT_TWO = math.sqrt(2.0)
F32, BF16 = jnp.float32, jnp.bfloat16


def make_filters(filter_taps):
    coeffs = filter_taps.astype(F32)
    signs = jnp.array([1.0, -1.0, 1.0, -1.0, 1.0], dtype=F32)
    lowpass = ROOT_TWO * coeffs[:, :, 0] / jnp.sum(coeffs[:, :, 0], axis=-1, keepdims=True)
    highpass = (
        signs
        * coeffs[:, :, 1]
        / jnp.sqrt(jnp.sum(coeffs[:, :, 1] * coeffs[:, :, 1], axis=-1, keepdims=True))
    )
    return jnp.stack([lowpass, highpass], axis=2)


def halves_of(x):
    high = x.astype(BF16)
    return high, (x - high.astype(F32)).astype(BF16)


def dot(a, b):
    return jnp.dot(a, b, preferred_element_type=F32)


def kernel(lats, taps, x_hbm, roots, out, *scratch):
    scratch = iter(scratch)

    def take(count):
        return [next(scratch) for _ in range(count)]

    xs = [take(LEVELS), take(LEVELS)]
    packs = [take(LEVELS - 1), take(LEVELS - 1)]
    lands = [take(LEVELS - 1), take(LEVELS - 1)]
    gs = [take(LEVELS), take(LEVELS)]
    ks = take(2)
    parts = take(LEVELS)
    hs, top = take(2)
    wmats, mats, sends, recvs, load_sem = scratch
    tile, lev, lanes = x_hbm.shape
    half = lanes // 2
    me = lax.axis_index("lat")
    has_down, has_up = me > 0, me < lats - 1
    above = {"lat": jnp.minimum(me + 1, lats - 1)}
    below = {"lat": jnp.maximum(me - 1, 0)}
    mesh_ids = pl.DeviceIdType.MESH
    slots = iter(range(10_000))
    pending = []

    def tap(level, direction, kind, k):
        return taps[((level * 2 + direction) * 2 + kind) * 5 + k]

    def exchange(src_up, dst_up, src_down, dst_down):
        up_slot, down_slot = next(slots), next(slots)
        up = pltpu.make_async_remote_copy(
            src_ref=src_up, dst_ref=dst_up, send_sem=sends.at[up_slot],
            recv_sem=recvs.at[up_slot], device_id=above, device_id_type=mesh_ids,
        )
        down = pltpu.make_async_remote_copy(
            src_ref=src_down, dst_ref=dst_down, send_sem=sends.at[down_slot],
            recv_sem=recvs.at[down_slot], device_id=below, device_id_type=mesh_ids,
        )

        @pl.when(has_up)
        def _():
            up.start()

        @pl.when(has_down)
        def _():
            down.start()

        def arrive():
            @pl.when(has_down)
            def _():
                up.wait_recv()

            @pl.when(has_up)
            def _():
                down.wait_recv()

        def sent():
            @pl.when(has_up)
            def _():
                up.wait_send()

            @pl.when(has_down)
            def _():
                down.wait_send()

        pending.append(sent)
        return arrive

    load = pltpu.make_async_copy(x_hbm, xs[0][0].at[pl.ds(2, tile)], load_sem)
    load.start()

    barrier = pltpu.get_barrier_semaphore()

    @pl.when(has_down)
    def _():
        pl.semaphore_signal(barrier, inc=1, device_id=below, device_id_type=mesh_ids)

    @pl.when(has_up)
    def _():
        pl.semaphore_signal(barrier, inc=1, device_id=above, device_id_type=mesh_ids)

    pl.semaphore_wait(barrier, has_down.astype(jnp.int32) + has_up.astype(jnp.int32))

    arrive = exchange(
        x_hbm.at[pl.ds(tile - 2, 2)], xs[0][0].at[pl.ds(0, 2)],
        x_hbm.at[pl.ds(0, 1)], xs[0][0].at[pl.ds(tile + 2, 1)],
    )

    def clear(ref, start, count):
        for r in range(count):
            ref[start + r] = jnp.zeros(ref.shape[1:], F32)

    edges_low, edges_high = [(xs[0][0], 0, 2)], [(xs[0][0], tile + 2, 1)]
    for t in range(2):
        for j in range(LEVELS):
            n = tile >> (j + 1)
            if j:
                edges_low.append((lands[t][j - 1], 0, 1))
                edges_high.append((xs[t][j], 2 * n + 2, 1))
            rim = 2 if t == 0 and j == 0 else 1
            edges_low.append((gs[t][j], 0, rim))
            edges_high.append((gs[t][j], n + rim, rim))
        rim = 2 - t
        edges_low.append((ks[t], 0, rim))
        edges_high.append((ks[t], tile // 2 + rim, rim))

    @pl.when(jnp.logical_not(has_down))
    def _():
        for edge in edges_low:
            clear(*edge)

    @pl.when(jnp.logical_not(has_up))
    def _():
        for edge in edges_high:
            clear(*edge)

    for j in range(LEVELS):
        width = lanes >> j
        block = lanes if j == 0 else half
        for flip in range(2):
            c = lax.broadcasted_iota(jnp.int32, (lanes, lanes), flip)
            o = lax.broadcasted_iota(jnp.int32, (lanes, lanes), 1 - flip)
            same = True
            if j:
                same = (c < half) == (o < half)
                c = jnp.where(c < half, c, c - half)
                o = jnp.where(o < half, o, o - half)
            is_low = o < width // 2
            t = c - 2 * jnp.where(is_low, o, o - width // 2) + 2
            w = jnp.zeros((lanes, lanes), F32)
            for k in range(5):
                w = jnp.where(t == k, jnp.where(is_low, tap(j, 1, 0, k), tap(j, 1, 1, k)), w)
            w = jnp.where((c < width) & (o < width) & same, w, 0.0)
            high, low = halves_of(w)
            at = 2 * j + flip
            wmats[at, pl.ds(0, lanes), pl.ds(0, lanes)] = high
            wmats[at, pl.ds(0, lanes), pl.ds(lanes, lanes)] = low
            wmats[at, pl.ds(lanes, lanes), pl.ds(0, lanes)] = high
            wmats[at, pl.ds(lanes, lanes), pl.ds(lanes, lanes)] = jnp.zeros_like(low)
    for b in range(roots.shape[0]):
        high, low = halves_of(roots[b])
        mats[b, pl.ds(0, lev)] = high
        mats[b, pl.ds(lev, lev)] = low

    def along_lon(x, at):
        high, low = halves_of(x)
        r = dot(jnp.concatenate([high, low], axis=1), wmats[at])
        return r[:, :lanes] + r[:, lanes:]

    def vertical(x, t, band):
        b = t * (LEVELS + 1) + band
        high, low = halves_of(x)
        r = dot(mats[b], high)
        return r[:lev] + r[lev:] + dot(mats[b, pl.ds(0, lev)], low)

    def loop(start, stop, body, step=2):
        count = max(stop - start, 0)
        whole = count // step
        if whole > 1:
            def several(i, _):
                for s in range(step):
                    body(start + i * step + s)
                return 0

            lax.fori_loop(0, whole, several, 0)
        else:
            whole = 0
        for i in range(start + whole * step, stop):
            body(i)

    lane = lax.broadcasted_iota(jnp.int32, (lev, lanes), 1)
    lane8 = lax.broadcasted_iota(jnp.int32, (8, lanes), 1)

    def swap(x):
        return pltpu.roll(x, half, 1)

    def twice(x):
        return jnp.where(lane < half, x, swap(x))

    def weighted(level, pairs):
        total = None
        for k, x in pairs:
            scale = jnp.where(lane8 < half, tap(level, 0, 0, k), tap(level, 0, 1, k))
            term = scale[None] * x.reshape(lev // 8, 8, lanes)
            total = term if total is None else total + term
        return total.reshape(lev, lanes)

    def analyse_first(t, i):
        rows = [xs[t][0][2 * i + k] for k in range(5)]
        low = sum(tap(0, 0, 0, k) * rows[k] for k in range(5))
        high = sum(tap(0, 0, 1, k) * rows[k] for k in range(5))
        both = along_lon(jnp.concatenate([low, high], axis=0), 0)
        parts[0][i] = both[:lev]
        hs[i] = both[lev:]
        xs[t][1][i + 2] = twice(both[:lev])

    def analyse(t, j, i):
        x = xs[t][j]
        part = along_lon(weighted(j, [(k, x[2 * i + k]) for k in range(5)]), 2 * j)
        parts[j][i] = part
        if j + 1 < LEVELS:
            xs[t][j + 1][i + 2] = twice(part)
        else:
            top[0] = part

    def share_coarse(t, j):
        rows, pack, land = xs[t][j], packs[t][j - 1], lands[t][j - 1]
        count = tile >> j
        pack[0] = jnp.where(lane < half, rows[count], rows[count + 1])
        wait = exchange(pack, land, rows.at[pl.ds(2, 1)], rows.at[pl.ds(count + 2, 1)])

        def arrived():
            wait()
            got = land[0]
            turned = swap(got)
            rows[0] = jnp.where(lane < half, got, turned)
            rows[1] = jnp.where(lane < half, turned, got)

        return arrived

    def share(ref, n, rim):
        return exchange(
            ref.at[pl.ds(n, rim)], ref.at[pl.ds(0, rim)],
            ref.at[pl.ds(rim, rim)], ref.at[pl.ds(n + rim, rim)],
        )

    def weigh_first(t, i):
        pair = vertical(jnp.concatenate([parts[0][i], hs[i]], axis=1), t, 0)
        parts[0][i] = pair[:, :lanes]
        ks[t][i + 2 - t] = along_lon(pair[:, lanes:], 1)

    def weigh(t, j):
        n = tile >> (j + 1)
        for i in range(0, n, 2):
            count = min(2, n - i)
            pair = [parts[j][i + s] for s in range(count)]
            pair = vertical(jnp.concatenate(pair, axis=1), t, j)
            for s in range(count):
                parts[j][i + s] = pair[:, s * lanes:(s + 1) * lanes]

    def lift(t, j, i, coarse):
        chosen = jnp.where(lane < (lanes >> (j + 1)), coarse, parts[j][i])
        rim = 2 if t == 0 and j == 0 else 1
        gs[t][j][i + rim] = along_lon(chosen, 2 * j + 1)

    def make(t, j, m):
        g = [gs[t][j][m + s] for s in range(3)]
        even = weighted(j, [(4 - 2 * s, g[s]) for s in range(3)])
        odd = weighted(j, [(5 - 2 * s, g[s]) for s in (1, 2)])
        return even + swap(even), odd + swap(odd)

    def make_first(t, m, even_only=False):
        rim = 2 - t
        g = [gs[t][0][m + rim + s] for s in (-1, 0, 1)]
        k = [ks[t][m + rim + s] for s in (-1, 0, 1)]
        even = sum(tap(0, 0, 0, 4 - 2 * s) * g[s] + tap(0, 0, 1, 4 - 2 * s) * k[s] for s in range(3))
        if even_only:
            return even
        odd = sum(tap(0, 0, 0, 5 - 2 * s) * g[s] + tap(0, 0, 1, 5 - 2 * s) * k[s] for s in (1, 2))
        return even, odd

    def middle(t):
        first_n = tile // 2
        arrived = share_coarse(t, 1)
        loop(0, first_n, lambda i: weigh_first(t, i))
        k_arrive = None
        for j in range(1, LEVELS):
            n = tile >> (j + 1)
            loop(1, n - 1, lambda i: analyse(t, j, i))
            arrived()
            analyse(t, j, 0)
            if n > 1:
                analyse(t, j, n - 1)
            if j + 1 < LEVELS:
                arrived = share_coarse(t, j + 1)
            if k_arrive is None:
                k_arrive = share(ks[t], first_n, 2 - t)
            if j + 1 < LEVELS:
                weigh(t, j)
        weigh(t, LEVELS - 1)
        lift(t, LEVELS - 1, 0, vertical(top[0], t, LEVELS))
        for j in reversed(range(1, LEVELS)):
            n = tile >> (j + 1)
            g_arrive = share(gs[t][j], n, 1)

            def both(m):
                even, odd = make(t, j, m)
                lift(t, j - 1, 2 * m, even)
                lift(t, j - 1, 2 * m + 1, odd)

            loop(1, n - 1, both, 1)
            g_arrive()
            both(0)
            if n > 1:
                both(n - 1)
        g_arrive = share(gs[t][0], first_n, 2 - t)

        def arrive_all():
            k_arrive()
            g_arrive()

        return arrive_all

    n = tile // 2
    load.wait()
    loop(1, n - 1, lambda i: analyse_first(0, i))
    arrive()
    analyse_first(0, 0)
    analyse_first(0, n - 1)
    arrive = middle(0)
    shaped = xs[1][0]

    def keep(m):
        shaped[2 * m + 2], shaped[2 * m + 3] = make_first(0, m)

    loop(1, n - 1, keep)
    loop(2, n - 2, lambda i: analyse_first(1, i))
    arrive()
    keep(0)
    keep(n - 1)
    even, odd = make_first(0, -1)
    inside = jnp.where(has_down, 1.0, 0.0).astype(F32)
    shaped[0], shaped[1] = inside * even, inside * odd
    shaped[tile + 2] = jnp.where(has_up, 1.0, 0.0).astype(F32) * make_first(0, n, even_only=True)
    for i in (0, 1, n - 2, n - 1):
        analyse_first(1, i)
    arrive = middle(1)

    def put(m):
        out[2 * m], out[2 * m + 1] = make_first(1, m)

    loop(1, n - 1, put)
    arrive()
    put(0)
    put(n - 1)
    for sent in pending:
        sent()


def on_device(increment, filter_taps, band_roots, lats):
    lev, tile, lanes = increment.shape
    padded = -(-lev // 16) * 16
    taps = make_filters(filter_taps).reshape(-1)
    x = jnp.pad(jnp.transpose(increment, (1, 0, 2)), ((0, 0), (0, padded - lev), (0, 0)))
    roots = jnp.pad(band_roots, ((0, 0), (0, padded - lev), (0, padded - lev)))
    roots = jnp.concatenate([roots, jnp.swapaxes(roots, 1, 2)])

    def slabs(count):
        return pltpu.VMEM((count, padded, lanes), F32)

    counts = [tile >> (j + 1) for j in range(LEVELS)]
    scratch = [slabs(2 * n + 3) for n in counts] * 2
    scratch += [slabs(1)] * (4 * (LEVELS - 1))
    scratch += [slabs(n + (4 if j == 0 else 2)) for j, n in enumerate(counts)]
    scratch += [slabs(n + 2) for n in counts]
    scratch += [slabs(counts[0] + 4), slabs(counts[0] + 2)]
    scratch += [slabs(n) for n in counts] + [slabs(counts[0]), slabs(1)]
    copies = 2 * (2 * LEVELS + 2 * (LEVELS - 1) + 3)
    scratch += [
        pltpu.VMEM((2 * LEVELS, 2 * lanes, 2 * lanes), BF16),
        pltpu.VMEM((2 * (LEVELS + 1), 2 * padded, padded), BF16),
        pltpu.SemaphoreType.DMA((copies,)),
        pltpu.SemaphoreType.DMA((copies,)),
        pltpu.SemaphoreType.DMA,
    ]
    y = pl.pallas_call(
        functools.partial(kernel, lats),
        out_shape=jax.ShapeDtypeStruct((tile, padded, lanes), F32),
        in_specs=[
            pl.BlockSpec(memory_space=pltpu.SMEM),
            pl.BlockSpec(memory_space=pl.ANY),
            pl.BlockSpec(memory_space=pltpu.VMEM),
        ],
        out_specs=pl.BlockSpec(memory_space=pltpu.VMEM),
        scratch_shapes=scratch,
        compiler_params=pltpu.CompilerParams(
            collective_id=0, has_side_effects=True, vmem_limit_bytes=48 << 20
        ),
    )(taps, x, roots)
    return jnp.transpose(y[:, :lev], (1, 0, 2))


def solution(mesh):
    placed = (P("member", "lat", None), P(), P())
    return jax.shard_map(
        functools.partial(on_device, lats=mesh.shape["lat"]),
        mesh=mesh, in_specs=placed, out_specs=P("member", "lat", None), check_vma=False,
    )
```

```python
import functools
import math

import jax
import jax.numpy as jnp
from jax import lax
from jax.experimental import pallas as pl
from jax.experimental.pallas import tpu as pltpu
from jax.sharding import PartitionSpec as P

LEVELS = 4
NEAR, NEAR_T, FAR, FAR_T = 5, 8, 12, 17
REACH = (1, -1, 2, -2, 3, -3)
ROOT_TWO = math.sqrt(2.0)
F32, BF16 = jnp.float32, jnp.bfloat16


def make_filters(filter_taps):
    coeffs = filter_taps.astype(F32)
    signs = jnp.array([1.0, -1.0, 1.0, -1.0, 1.0], dtype=F32)
    lowpass = ROOT_TWO * coeffs[:, :, 0] / jnp.sum(coeffs[:, :, 0], axis=-1, keepdims=True)
    highpass = (
        signs
        * coeffs[:, :, 1]
        / jnp.sqrt(jnp.sum(coeffs[:, :, 1] * coeffs[:, :, 1], axis=-1, keepdims=True))
    )
    return jnp.stack([lowpass, highpass], axis=2)


def halves_of(x):
    high = x.astype(BF16)
    return high, (x - high.astype(F32)).astype(BF16)


def dot(a, b):
    return jnp.dot(a, b, preferred_element_type=F32)


def kernel(lats, taps, x_hbm, roots, out, *scratch):
    scratch = iter(scratch)

    def take(count):
        return [next(scratch) for _ in range(count)]

    xs = [take(2), take(2)]
    packs, lands = take(2), take(2)
    wides, seconds = take(2), take(2)
    gs, ks = take(2), take(2)
    g_second, part, hs, cats = take(4)
    wmats, mats, sends, recvs, load_sem = scratch
    tile, lev, lanes = x_hbm.shape
    half = lanes // 2
    me = lax.axis_index("lat")
    has_down, has_up = me > 0, me < lats - 1
    mesh_ids = pl.DeviceIdType.MESH
    slots = iter(range(10_000))
    pending = []

    def tap(level, direction, kind, k):
        return taps[((level * 2 + direction) * 2 + kind) * 5 + k]

    def device(d):
        return {"lat": jnp.clip(me + d, 0, lats - 1)}

    def there(d):
        return me + d < lats if d > 0 else me + d >= 0

    def exchange(moves):
        waits = []
        for d, src, dst in moves:
            slot = next(slots)
            copy = pltpu.make_async_remote_copy(
                src_ref=src, dst_ref=dst, send_sem=sends.at[slot],
                recv_sem=recvs.at[slot], device_id=device(d), device_id_type=mesh_ids,
            )
            waits.append((d, copy))
            pl.when(there(d))(copy.start)
            pending.append(lambda d=d, copy=copy: pl.when(there(d))(copy.wait_send))

        def arrive():
            for d, copy in waits:
                pl.when(there(-d))(copy.wait_recv)

        return arrive

    load = pltpu.make_async_copy(x_hbm, xs[0][0].at[pl.ds(2, tile)], load_sem)
    load.start()

    barrier = pltpu.get_barrier_semaphore()

    peers = 0
    for d in REACH:
        def greet(d=d):
            pl.semaphore_signal(barrier, inc=1, device_id=device(d), device_id_type=mesh_ids)

        pl.when(there(d))(greet)
        peers = peers + there(d).astype(jnp.int32)
    pl.semaphore_wait(barrier, peers)

    arrive = exchange([
        (1, x_hbm.at[pl.ds(tile - 2, 2)], xs[0][0].at[pl.ds(0, 2)]),
        (-1, x_hbm.at[pl.ds(0, 1)], xs[0][0].at[pl.ds(tile + 2, 1)]),
    ])

    def clear(ref, start, count):
        for r in range(count):
            ref[start + r] = jnp.zeros(ref.shape[1:], F32)

    half_rows, quarter = tile // 2, tile // 4
    edges_low, edges_high = [(xs[0][0], 0, 2)], [(xs[0][0], tile + 2, 1)]
    for t in range(2):
        rim = 2 - t
        edges_low += [(lands[t], 0, 1), (gs[t], 0, rim), (ks[t], 0, rim), (seconds[t], 0, 1)]
        edges_high += [(xs[t][1], half_rows + 2, 1), (gs[t], half_rows + rim, rim)]
        edges_high += [(ks[t], half_rows + rim, rim), (seconds[t], quarter + 1, 1)]

    @pl.when(jnp.logical_not(has_down))
    def _():
        for edge in edges_low:
            clear(*edge)

    @pl.when(jnp.logical_not(has_up))
    def _():
        for edge in edges_high:
            clear(*edge)

    for d in REACH:
        def blank(d=d):
            for t in range(2):
                clear(wides[t], 3 + d, 1)

        pl.when(jnp.logical_not(there(d)))(blank)
    cats[7] = jnp.zeros(cats.shape[1:], BF16)

    def keep_matrix(at, w):
        high, low = halves_of(w)
        wmats[at, pl.ds(0, lanes), pl.ds(0, lanes)] = high
        wmats[at, pl.ds(0, lanes), pl.ds(lanes, lanes)] = low
        wmats[at, pl.ds(lanes, lanes), pl.ds(0, lanes)] = high
        wmats[at, pl.ds(lanes, lanes), pl.ds(lanes, lanes)] = jnp.zeros_like(low)

    def build_wide(at, level, shift, flip):
        width = lanes >> level
        c = lax.broadcasted_iota(jnp.int32, (lanes, lanes), flip)
        o = lax.broadcasted_iota(jnp.int32, (lanes, lanes), 1 - flip)
        pitch = width if level == 2 else 4 * width
        row, col = c // pitch, c % pitch
        out_row, kind, out_col = o // (2 * width), (o // width) % 2, o % width
        is_low = out_col < width // 2
        t = col - 2 * jnp.where(is_low, out_col, out_col - width // 2) + 2
        u = row + shift - 2 * out_row + 2
        lon = jnp.zeros((lanes, lanes), F32)
        lat = jnp.zeros((lanes, lanes), F32)
        for k in range(5):
            lon = jnp.where(t == k, jnp.where(is_low, tap(level, 1, 0, k), tap(level, 1, 1, k)), lon)
            lat = jnp.where(u == k, jnp.where(kind == 0, tap(level, 0, 0, k), tap(level, 0, 1, k)), lat)
        keep_matrix(at, jnp.where(col < width, lon * lat, 0.0))

    def build_second():
        for q in (-1, 0, 1):
            build_wide(NEAR + q, 2, 4 * q, 0)
            build_wide(NEAR_T + q, 2, 4 * q, 1)

    def build_third():
        for q in range(-2, 4):
            build_wide(FAR + q, 3, 2 * q + 2, 0)
            if -2 < q < 2:
                build_wide(FAR_T + q, 3, 2 * q + 2, 1)

    for j in range(2):
        width = lanes >> j
        block = lanes if j == 0 else half
        for flip in range(2):
            c = lax.broadcasted_iota(jnp.int32, (lanes, lanes), flip)
            o = lax.broadcasted_iota(jnp.int32, (lanes, lanes), 1 - flip)
            same = True
            if j:
                same = (c < half) == (o < half)
                c = jnp.where(c < half, c, c - half)
                o = jnp.where(o < half, o, o - half)
            is_low = o < width // 2
            t = c - 2 * jnp.where(is_low, o, o - width // 2) + 2
            w = jnp.zeros((lanes, lanes), F32)
            for k in range(5):
                w = jnp.where(t == k, jnp.where(is_low, tap(j, 1, 0, k), tap(j, 1, 1, k)), w)
            w = jnp.where((c < width) & (o < width) & same, w, 0.0)
            keep_matrix(2 * j + flip, w)
    for b in range(roots.shape[0]):
        high, low = halves_of(roots[b])
        mats[b, pl.ds(0, lev)] = high
        mats[b, pl.ds(lev, lev)] = low

    def along_lon(x, at):
        high, low = halves_of(x)
        r = dot(jnp.concatenate([high, low], axis=1), wmats[at])
        return r[:, :lanes] + r[:, lanes:]

    def vertical(x, t, band):
        b = t * (LEVELS + 1) + band
        high, low = halves_of(x)
        r = dot(mats[b], high)
        return r[:lev] + r[lev:] + dot(mats[b, pl.ds(0, lev)], low)

    def loop(start, stop, body, step=2):
        count = max(stop - start, 0)
        whole = count // step
        if whole > 1:
            def several(i, _):
                for s in range(step):
                    body(start + i * step + s)
                return 0

            lax.fori_loop(0, whole, several, 0)
        else:
            whole = 0
        for i in range(start + whole * step, stop):
            body(i)

    lane = lax.broadcasted_iota(jnp.int32, (lev, lanes), 1)
    lane8 = lax.broadcasted_iota(jnp.int32, (8, lanes), 1)

    def swap(x):
        return pltpu.roll(x, half, 1)

    def twice(x):
        return jnp.where(lane < half, x, swap(x))

    def weighted(level, pairs):
        total = None
        for k, x in pairs:
            scale = jnp.where(lane8 < half, tap(level, 0, 0, k), tap(level, 0, 1, k))
            term = scale[None] * x.reshape(lev // 8, 8, lanes)
            total = term if total is None else total + term
        return total.reshape(lev, lanes)

    def analyse_first(t, i):
        rows = [xs[t][0][2 * i + k] for k in range(5)]
        low = sum(tap(0, 0, 0, k) * rows[k] for k in range(5))
        high = sum(tap(0, 0, 1, k) * rows[k] for k in range(5))
        both = along_lon(jnp.concatenate([low, high], axis=0), 0)
        part[i] = both[:lev]
        hs[i] = both[lev:]
        xs[t][1][i + 2] = twice(both[:lev])

    def analyse(t, i):
        rows = [(k, xs[t][1][2 * i + k]) for k in range(5)]
        seconds[t][i + 1] = along_lon(weighted(1, rows), 2)

    def share_coarse(t):
        rows, pack, land = xs[t][1], packs[t], lands[t]
        pack[0] = jnp.where(lane < half, rows[half_rows], rows[half_rows + 1])
        wait = exchange([
            (1, pack, land),
            (-1, rows.at[pl.ds(2, 1)], rows.at[pl.ds(half_rows + 2, 1)]),
        ])

        def arrived():
            wait()
            got = land[0]
            turned = swap(got)
            rows[0] = jnp.where(lane < half, got, turned)
            rows[1] = jnp.where(lane < half, turned, got)

        return arrived

    def share(ref, n, rim):
        return exchange([
            (1, ref.at[pl.ds(n, rim)], ref.at[pl.ds(0, rim)]),
            (-1, ref.at[pl.ds(rim, rim)], ref.at[pl.ds(n + rim, rim)]),
        ])

    def weigh_first(t, i):
        pair = vertical(jnp.concatenate([part[i], hs[i]], axis=1), t, 0)
        part[i] = pair[:, :lanes]
        ks[t][i + 2 - t] = along_lon(pair[:, lanes:], 1)

    def weigh_second(t):
        for i in range(0, quarter, 2):
            pair = [seconds[t][i + s + 1] for s in range(2)]
            pair = vertical(jnp.concatenate(pair, axis=1), t, 1)
            for s in range(2):
                seconds[t][i + s + 1] = pair[:, s * lanes:(s + 1) * lanes]

    def lift_second(t, i, coarse):
        chosen = jnp.where(lane < lanes // 4, coarse, seconds[t][i + 1])
        return along_lon(chosen, 3)

    def lift_first(t, i, coarse):
        chosen = jnp.where(lane < half, coarse, part[i])
        gs[t][i + 2 - t] = along_lon(chosen, 1)

    def make(m):
        g = [g_second[m + s] for s in range(3)]
        even = weighted(1, [(4 - 2 * s, g[s]) for s in range(3)])
        odd = weighted(1, [(5 - 2 * s, g[s]) for s in (1, 2)])
        return even + swap(even), odd + swap(odd)

    def make_first(t, m, even_only=False):
        rim = 2 - t
        g = [gs[t][m + rim + s] for s in (-1, 0, 1)]
        k = [ks[t][m + rim + s] for s in (-1, 0, 1)]
        even = sum(tap(0, 0, 0, 4 - 2 * s) * g[s] + tap(0, 0, 1, 4 - 2 * s) * k[s] for s in range(3))
        if even_only:
            return even
        odd = sum(tap(0, 0, 0, 5 - 2 * s) * g[s] + tap(0, 0, 1, 5 - 2 * s) * k[s] for s in (1, 2))
        return even, odd

    def joined(x):
        return jnp.concatenate(halves_of(x), axis=1)

    def folded(r):
        return r[:, :lanes] + r[:, lanes:]

    def present(s):
        return jnp.where((me + s >= 0) & (me + s < lats), 1.0, 0.0).astype(F32)

    def cat_rows(start, count):
        return cats[pl.ds(start, count)].reshape(count * lev, 2 * lanes)

    def deep(t):
        for s in range(7):
            cats[s] = joined(wides[t][s])
        q = dot(cat_rows(1, 6), wmats[NEAR])
        q = folded(q + dot(cat_rows(0, 6), wmats[NEAR - 1]) + dot(cat_rows(2, 6), wmats[NEAR + 1]))
        q = [present(s - 2) * q[s * lev:(s + 1) * lev] for s in range(6)]
        third = folded(sum(dot(joined(q[s]), wmats[FAR + s - 2]) for s in range(6)))
        owner = me + lane // (lanes // 4) - 1
        third = jnp.where((owner >= 0) & (owner < lats), third, 0.0)
        top = vertical(third, t, LEVELS)
        third = jnp.where(lane % (lanes // 4) < lanes // 16, top, vertical(third, t, 3))
        third = joined(third)
        second = vertical(jnp.concatenate(q[1:4], axis=1), t, 2)
        lifted = []
        for s in (-1, 0, 1):
            c = folded(dot(third, wmats[FAR_T + s]))
            d = second[:, (s + 1) * lanes:(s + 2) * lanes]
            lifted.append(joined(present(s) * jnp.where(lane % half < lanes // 8, c, d)))

        def spread(pairs):
            return folded(sum(dot(lifted[s + 1], wmats[NEAR_T + d]) for s, d in pairs))

        return (
            spread(((-1, 0), (0, -1))),
            spread(((-1, 1), (0, 0), (1, -1))),
            spread(((0, 1), (1, 0))),
        )

    def middle(t):
        arrived = share_coarse(t)
        if t == 0:
            build_second()
        loop(0, half_rows, lambda i: weigh_first(t, i))
        loop(1, quarter - 1, lambda i: analyse(t, i))
        arrived()
        analyse(t, 0)
        analyse(t, quarter - 1)
        own = seconds[t][1]
        for r in range(1, quarter):
            turned = pltpu.roll(seconds[t][r + 1], r * (lanes // 4), 1)
            own = jnp.where(lane < r * (lanes // 4), own, turned)
        wide = wides[t]
        wide[3] = own
        arrived = exchange([(d, wide.at[pl.ds(3, 1)], wide.at[pl.ds(3 - d, 1)]) for d in REACH])
        weigh_second(t)
        second_arrive = share(seconds[t], quarter, 1)
        k_arrive = share(ks[t], half_rows, 2 - t)
        if t == 0:
            build_third()
        arrived()
        before, own, after = deep(t)
        for r in range(quarter):
            coarse = own if r == 0 else pltpu.roll(own, lanes - r * (lanes // 4), 1)
            g_second[r + 1] = lift_second(t, r, coarse)

        def both(m):
            even, odd = make(m)
            lift_first(t, 2 * m, even)
            lift_first(t, 2 * m + 1, odd)

        second_arrive()
        before = pltpu.roll(before, lanes // 4, 1)
        g_second[0] = present(-1) * lift_second(t, -1, before)
        g_second[quarter + 1] = present(1) * lift_second(t, quarter, after)
        both(0)
        both(quarter - 1)
        g_arrive = share(gs[t], half_rows, 2 - t)
        loop(1, quarter - 1, both, 1)

        def arrive_all():
            k_arrive()
            g_arrive()

        return arrive_all

    n = tile // 2
    load.wait()
    loop(1, n - 1, lambda i: analyse_first(0, i))
    arrive()
    analyse_first(0, 0)
    analyse_first(0, n - 1)
    arrive = middle(0)
    shaped = xs[1][0]

    def keep(m):
        shaped[2 * m + 2], shaped[2 * m + 3] = make_first(0, m)

    loop(1, n - 1, keep)
    loop(2, n - 2, lambda i: analyse_first(1, i))
    arrive()
    keep(0)
    keep(n - 1)
    even, odd = make_first(0, -1)
    inside = jnp.where(has_down, 1.0, 0.0).astype(F32)
    shaped[0], shaped[1] = inside * even, inside * odd
    shaped[tile + 2] = jnp.where(has_up, 1.0, 0.0).astype(F32) * make_first(0, n, even_only=True)
    for i in (0, 1, n - 2, n - 1):
        analyse_first(1, i)
    arrive = middle(1)

    def put(m):
        out[2 * m], out[2 * m + 1] = make_first(1, m)

    loop(1, n - 1, put)
    arrive()
    put(0)
    put(n - 1)
    for sent in pending:
        sent()


def on_device(increment, filter_taps, band_roots, lats):
    lev, tile, lanes = increment.shape
    padded = -(-lev // 16) * 16
    taps = make_filters(filter_taps).reshape(-1)
    x = jnp.pad(jnp.transpose(increment, (1, 0, 2)), ((0, 0), (0, padded - lev), (0, 0)))
    roots = jnp.pad(band_roots, ((0, 0), (0, padded - lev), (0, padded - lev)))
    roots = jnp.concatenate([roots, jnp.swapaxes(roots, 1, 2)])

    def slabs(count):
        return pltpu.VMEM((count, padded, lanes), F32)

    counts = [tile >> (j + 1) for j in range(LEVELS)]
    scratch = [slabs(2 * n + 3) for n in counts[:2]] * 2
    scratch += [slabs(1)] * 4 + [slabs(7)] * 2 + [slabs(counts[1] + 2)] * 2
    scratch += [slabs(counts[0] + 4), slabs(counts[0] + 2)] * 2
    scratch += [slabs(counts[1] + 2), slabs(counts[0]), slabs(counts[0])]
    scratch += [pltpu.VMEM((8, padded, 2 * lanes), BF16)]
    copies = 2 + 2 * (2 + len(REACH) + 2 * 3)
    scratch += [
        pltpu.VMEM((FAR_T + 2, 2 * lanes, 2 * lanes), BF16),
        pltpu.VMEM((2 * (LEVELS + 1), 2 * padded, padded), BF16),
        pltpu.SemaphoreType.DMA((copies,)),
        pltpu.SemaphoreType.DMA((copies,)),
        pltpu.SemaphoreType.DMA,
    ]
    y = pl.pallas_call(
        functools.partial(kernel, lats),
        out_shape=jax.ShapeDtypeStruct((tile, padded, lanes), F32),
        in_specs=[
            pl.BlockSpec(memory_space=pltpu.SMEM),
            pl.BlockSpec(memory_space=pl.ANY),
            pl.BlockSpec(memory_space=pltpu.VMEM),
        ],
        out_specs=pl.BlockSpec(memory_space=pltpu.VMEM),
        scratch_shapes=scratch,
        compiler_params=pltpu.CompilerParams(
            collective_id=0, has_side_effects=True, vmem_limit_bytes=48 << 20
        ),
    )(taps, x, roots)
    return jnp.transpose(y[:, :lev], (1, 0, 2))


def solution(mesh):
    placed = (P("member", "lat", None), P(), P())
    return jax.shard_map(
        functools.partial(on_device, lats=mesh.shape["lat"]),
        mesh=mesh, in_specs=placed, out_specs=P("member", "lat", None), check_vma=False,
    )
```

```python
import functools
import math

import jax
import jax.numpy as jnp
from jax import lax
from jax.experimental import pallas as pl
from jax.experimental.pallas import tpu as pltpu
from jax.sharding import PartitionSpec as P

LEVELS = 4
NEAR, NEAR_T, FAR, FAR_T = 5, 8, 12, 17
REACH = (1, -1, 2, -2, 3, -3)
ROOT_TWO = math.sqrt(2.0)
F32, BF16 = jnp.float32, jnp.bfloat16


def halves_of(x):
    high = x.astype(BF16)
    return high, (x - high.astype(F32)).astype(BF16)


def dot(a, b):
    return jnp.dot(a, b, preferred_element_type=F32)


def kernel(lats, raw_taps, x_hbm, roots_hbm, out, *scratch):
    scratch = iter(scratch)

    def take(count):
        return [next(scratch) for _ in range(count)]

    xs = [take(2), take(2)]
    packs, lands = take(2), take(2)
    wides, seconds = take(2), take(2)
    gs, ks = take(2), take(2)
    g_second, part, hs, cats = take(4)
    wmats, mats, taps, roots, square, sends, recvs, load_sem, root_sem = scratch
    tile, lev, lanes = x_hbm.shape
    half = lanes // 2
    me = lax.axis_index("lat")
    has_down, has_up = me > 0, me < lats - 1
    mesh_ids = pl.DeviceIdType.MESH
    slots = iter(range(10_000))
    pending = []

    def tap(level, direction, kind, k):
        return taps[((level * 2 + direction) * 2 + kind) * 5 + k]

    def device(d):
        return {"lat": jnp.clip(me + d, 0, lats - 1)}

    def there(d):
        return me + d < lats if d > 0 else me + d >= 0

    def exchange(moves):
        waits = []
        for d, src, dst in moves:
            slot = next(slots)
            copy = pltpu.make_async_remote_copy(
                src_ref=src, dst_ref=dst, send_sem=sends.at[slot],
                recv_sem=recvs.at[slot], device_id=device(d), device_id_type=mesh_ids,
            )
            waits.append((d, copy))
            pl.when(there(d))(copy.start)
            pending.append(lambda d=d, copy=copy: pl.when(there(d))(copy.wait_send))

        def arrive():
            for d, copy in waits:
                pl.when(there(-d))(copy.wait_recv)

        return arrive

    load = pltpu.make_async_copy(x_hbm, xs[0][0].at[pl.ds(2, tile)], load_sem)
    load.start()
    fetch = pltpu.make_async_copy(roots_hbm, roots, root_sem)
    fetch.start()

    barrier = pltpu.get_barrier_semaphore()

    peers = 0
    for d in REACH:
        def greet(d=d):
            pl.semaphore_signal(barrier, inc=1, device_id=device(d), device_id_type=mesh_ids)

        pl.when(there(d))(greet)
        peers = peers + there(d).astype(jnp.int32)
    pl.semaphore_wait(barrier, peers)

    arrive = exchange([
        (1, x_hbm.at[pl.ds(tile - 2, 2)], xs[0][0].at[pl.ds(0, 2)]),
        (-1, x_hbm.at[pl.ds(0, 1)], xs[0][0].at[pl.ds(tile + 2, 1)]),
    ])

    for f in range(4 * LEVELS):
        values = [raw_taps[f * 5 + k].astype(F32) for k in range(5)]
        if f % 2:
            total = jnp.full((8, lanes), sum(v * v for v in values), F32)
            scale = (1.0 / jnp.sqrt(total))[0, 0]
        else:
            scale = (ROOT_TWO / jnp.full((8, lanes), sum(values), F32))[0, 0]
        for k in range(5):
            taps[f * 5 + k] = values[k] * (-scale if f % 2 and k % 2 else scale)

    def clear(ref, start, count):
        for r in range(count):
            ref[start + r] = jnp.zeros(ref.shape[1:], F32)

    half_rows, quarter = tile // 2, tile // 4
    edges_low, edges_high = [(xs[0][0], 0, 2)], [(xs[0][0], tile + 2, 1)]
    for t in range(2):
        rim = 2 - t
        edges_low += [(lands[t], 0, 1), (gs[t], 0, rim), (ks[t], 0, rim), (seconds[t], 0, 1)]
        edges_high += [(xs[t][1], half_rows + 2, 1), (gs[t], half_rows + rim, rim)]
        edges_high += [(ks[t], half_rows + rim, rim), (seconds[t], quarter + 1, 1)]

    @pl.when(jnp.logical_not(has_down))
    def _():
        for edge in edges_low:
            clear(*edge)

    @pl.when(jnp.logical_not(has_up))
    def _():
        for edge in edges_high:
            clear(*edge)

    for d in REACH:
        def blank(d=d):
            for t in range(2):
                clear(wides[t], 3 + d, 1)

        pl.when(jnp.logical_not(there(d)))(blank)
    cats[7] = jnp.zeros(cats.shape[1:], BF16)

    def keep_matrix(at, w):
        high, low = halves_of(w)
        wmats[at, pl.ds(0, lanes), pl.ds(0, lanes)] = high
        wmats[at, pl.ds(0, lanes), pl.ds(lanes, lanes)] = low
        wmats[at, pl.ds(lanes, lanes), pl.ds(0, lanes)] = high
        wmats[at, pl.ds(lanes, lanes), pl.ds(lanes, lanes)] = jnp.zeros_like(low)

    def build_wide(at, level, shift, flip):
        width = lanes >> level
        c = lax.broadcasted_iota(jnp.int32, (lanes, lanes), flip)
        o = lax.broadcasted_iota(jnp.int32, (lanes, lanes), 1 - flip)
        pitch = width if level == 2 else 4 * width
        row, col = c // pitch, c % pitch
        out_row, kind, out_col = o // (2 * width), (o // width) % 2, o % width
        is_low = out_col < width // 2
        t = col - 2 * jnp.where(is_low, out_col, out_col - width // 2) + 2
        u = row + shift - 2 * out_row + 2
        lon = jnp.zeros((lanes, lanes), F32)
        lat = jnp.zeros((lanes, lanes), F32)
        for k in range(5):
            lon = jnp.where(t == k, jnp.where(is_low, tap(level, 1, 0, k), tap(level, 1, 1, k)), lon)
            lat = jnp.where(u == k, jnp.where(kind == 0, tap(level, 0, 0, k), tap(level, 0, 1, k)), lat)
        keep_matrix(at, jnp.where(col < width, lon * lat, 0.0))

    def build_second():
        for q in (-1, 0, 1):
            build_wide(NEAR + q, 2, 4 * q, 0)
            build_wide(NEAR_T + q, 2, 4 * q, 1)

    def build_third():
        for q in range(-2, 4):
            build_wide(FAR + q, 3, 2 * q + 2, 0)
            if -2 < q < 2:
                build_wide(FAR_T + q, 3, 2 * q + 2, 1)

    for j in range(2):
        width = lanes >> j
        block = lanes if j == 0 else half
        for flip in range(2):
            c = lax.broadcasted_iota(jnp.int32, (lanes, lanes), flip)
            o = lax.broadcasted_iota(jnp.int32, (lanes, lanes), 1 - flip)
            same = True
            if j:
                same = (c < half) == (o < half)
                c = jnp.where(c < half, c, c - half)
                o = jnp.where(o < half, o, o - half)
            is_low = o < width // 2
            t = c - 2 * jnp.where(is_low, o, o - width // 2) + 2
            w = jnp.zeros((lanes, lanes), F32)
            for k in range(5):
                w = jnp.where(t == k, jnp.where(is_low, tap(j, 1, 0, k), tap(j, 1, 1, k)), w)
            w = jnp.where((c < width) & (o < width) & same, w, 0.0)
            keep_matrix(2 * j + flip, w)
    fetch.wait()
    square[...] = jnp.zeros(square.shape, F32)
    count = roots.shape[1]
    for b in range(LEVELS + 1):
        square[pl.ds(0, count), pl.ds(0, count)] = roots[b]
        whole = square[...]
        for t, m in enumerate((whole, whole.T)):
            high, low = halves_of(m[:lev, :lev])
            mats[t * (LEVELS + 1) + b, pl.ds(0, lev)] = high
            mats[t * (LEVELS + 1) + b, pl.ds(lev, lev)] = low

    def along_lon(x, at):
        high, low = halves_of(x)
        r = dot(jnp.concatenate([high, low], axis=1), wmats[at])
        return r[:, :lanes] + r[:, lanes:]

    def vertical(x, t, band):
        b = t * (LEVELS + 1) + band
        high, low = halves_of(x)
        r = dot(mats[b], high)
        return r[:lev] + r[lev:] + dot(mats[b, pl.ds(0, lev)], low)

    def loop(start, stop, body, step=2):
        count = max(stop - start, 0)
        whole = count // step
        if whole > 1:
            def several(i, _):
                for s in range(step):
                    body(start + i * step + s)
                return 0

            lax.fori_loop(0, whole, several, 0)
        else:
            whole = 0
        for i in range(start + whole * step, stop):
            body(i)

    lane = lax.broadcasted_iota(jnp.int32, (lev, lanes), 1)
    lane8 = lax.broadcasted_iota(jnp.int32, (8, lanes), 1)

    def swap(x):
        return pltpu.roll(x, half, 1)

    def twice(x):
        return jnp.where(lane < half, x, swap(x))

    def weighted(level, pairs):
        total = None
        for k, x in pairs:
            scale = jnp.where(lane8 < half, tap(level, 0, 0, k), tap(level, 0, 1, k))
            term = scale[None] * x.reshape(lev // 8, 8, lanes)
            total = term if total is None else total + term
        return total.reshape(lev, lanes)

    def analyse_first(t, i):
        rows = [xs[t][0][2 * i + k] for k in range(5)]
        low = sum(tap(0, 0, 0, k) * rows[k] for k in range(5))
        high = sum(tap(0, 0, 1, k) * rows[k] for k in range(5))
        both = along_lon(jnp.concatenate([low, high], axis=0), 0)
        part[i] = both[:lev]
        hs[i] = both[lev:]
        xs[t][1][i + 2] = twice(both[:lev])

    def analyse(t, i):
        rows = [(k, xs[t][1][2 * i + k]) for k in range(5)]
        seconds[t][i + 1] = along_lon(weighted(1, rows), 2)

    def share_coarse(t):
        rows, pack, land = xs[t][1], packs[t], lands[t]
        pack[0] = jnp.where(lane < half, rows[half_rows], rows[half_rows + 1])
        wait = exchange([
            (1, pack, land),
            (-1, rows.at[pl.ds(2, 1)], rows.at[pl.ds(half_rows + 2, 1)]),
        ])

        def arrived():
            wait()
            got = land[0]
            turned = swap(got)
            rows[0] = jnp.where(lane < half, got, turned)
            rows[1] = jnp.where(lane < half, turned, got)

        return arrived

    def share(ref, n, rim):
        return exchange([
            (1, ref.at[pl.ds(n, rim)], ref.at[pl.ds(0, rim)]),
            (-1, ref.at[pl.ds(rim, rim)], ref.at[pl.ds(n + rim, rim)]),
        ])

    def weigh_first(t, i):
        pair = vertical(jnp.concatenate([part[i], hs[i]], axis=1), t, 0)
        part[i] = pair[:, :lanes]
        ks[t][i + 2 - t] = along_lon(pair[:, lanes:], 1)

    def weigh_second(t):
        for i in range(0, quarter, 2):
            pair = [seconds[t][i + s + 1] for s in range(2)]
            pair = vertical(jnp.concatenate(pair, axis=1), t, 1)
            for s in range(2):
                seconds[t][i + s + 1] = pair[:, s * lanes:(s + 1) * lanes]

    def lift_second(t, i, coarse):
        chosen = jnp.where(lane < lanes // 4, coarse, seconds[t][i + 1])
        return along_lon(chosen, 3)

    def lift_first(t, i, coarse):
        chosen = jnp.where(lane < half, coarse, part[i])
        gs[t][i + 2 - t] = along_lon(chosen, 1)

    def make(m):
        g = [g_second[m + s] for s in range(3)]
        even = weighted(1, [(4 - 2 * s, g[s]) for s in range(3)])
        odd = weighted(1, [(5 - 2 * s, g[s]) for s in (1, 2)])
        return even + swap(even), odd + swap(odd)

    def make_first(t, m, even_only=False):
        rim = 2 - t
        g = [gs[t][m + rim + s] for s in (-1, 0, 1)]
        k = [ks[t][m + rim + s] for s in (-1, 0, 1)]
        even = sum(tap(0, 0, 0, 4 - 2 * s) * g[s] + tap(0, 0, 1, 4 - 2 * s) * k[s] for s in range(3))
        if even_only:
            return even
        odd = sum(tap(0, 0, 0, 5 - 2 * s) * g[s] + tap(0, 0, 1, 5 - 2 * s) * k[s] for s in (1, 2))
        return even, odd

    def joined(x):
        return jnp.concatenate(halves_of(x), axis=1)

    def folded(r):
        return r[:, :lanes] + r[:, lanes:]

    def present(s):
        return jnp.where((me + s >= 0) & (me + s < lats), 1.0, 0.0).astype(F32)

    def cat_rows(start, count):
        return cats[pl.ds(start, count)].reshape(count * lev, 2 * lanes)

    def deep(t, near_arrive, far_arrive):
        def coarsen(start, count):
            q = dot(cat_rows(start, count), wmats[NEAR])
            q = q + dot(cat_rows(start - 1, count), wmats[NEAR - 1])
            q = folded(q + dot(cat_rows(start + 1, count), wmats[NEAR + 1]))
            return [present(start + s - 3) * q[s * lev:(s + 1) * lev] for s in range(count)]

        near_arrive()
        for s in range(1, 6):
            cats[s] = joined(wides[t][s])
        middle_q = coarsen(2, 3)
        second = vertical(jnp.concatenate(middle_q, axis=1), t, 2)
        partial = sum(dot(joined(middle_q[s]), wmats[FAR + s - 1]) for s in range(3))
        far_arrive()
        for s in (0, 6):
            cats[s] = joined(wides[t][s])
        q = coarsen(1, 1) + middle_q + coarsen(5, 2)
        third = folded(partial + sum(dot(joined(q[s]), wmats[FAR + s - 2]) for s in (0, 4, 5)))
        owner = me + lane // (lanes // 4) - 1
        third = jnp.where((owner >= 0) & (owner < lats), third, 0.0)
        top = vertical(third, t, LEVELS)
        third = jnp.where(lane % (lanes // 4) < lanes // 16, top, vertical(third, t, 3))
        third = joined(third)
        lifted = []
        for s in (-1, 0, 1):
            c = folded(dot(third, wmats[FAR_T + s]))
            d = second[:, (s + 1) * lanes:(s + 2) * lanes]
            lifted.append(joined(present(s) * jnp.where(lane % half < lanes // 8, c, d)))

        def spread(pairs):
            return folded(sum(dot(lifted[s + 1], wmats[NEAR_T + d]) for s, d in pairs))

        return (
            spread(((-1, 0), (0, -1))),
            spread(((-1, 1), (0, 0), (1, -1))),
            spread(((0, 1), (1, 0))),
        )

    def middle(t):
        arrived = share_coarse(t)
        if t == 0:
            build_second()
        loop(0, half_rows, lambda i: weigh_first(t, i))
        loop(1, quarter - 1, lambda i: analyse(t, i))
        arrived()
        analyse(t, 0)
        analyse(t, quarter - 1)
        own = seconds[t][1]
        for r in range(1, quarter):
            turned = pltpu.roll(seconds[t][r + 1], r * (lanes // 4), 1)
            own = jnp.where(lane < r * (lanes // 4), own, turned)
        wide = wides[t]
        wide[3] = own
        moves = [(d, wide.at[pl.ds(3, 1)], wide.at[pl.ds(3 - d, 1)]) for d in REACH]
        near_arrive, far_arrive = exchange(moves[:4]), exchange(moves[4:])
        weigh_second(t)
        second_arrive = share(seconds[t], quarter, 1)
        if t == 0:
            build_third()
        before, own, after = deep(t, near_arrive, far_arrive)
        k_arrive = share(ks[t], half_rows, 2 - t)
        for r in range(quarter):
            coarse = own if r == 0 else pltpu.roll(own, lanes - r * (lanes // 4), 1)
            g_second[r + 1] = lift_second(t, r, coarse)

        def both(m):
            even, odd = make(m)
            lift_first(t, 2 * m, even)
            lift_first(t, 2 * m + 1, odd)

        second_arrive()
        before = pltpu.roll(before, lanes // 4, 1)
        g_second[0] = present(-1) * lift_second(t, -1, before)
        g_second[quarter + 1] = present(1) * lift_second(t, quarter, after)
        both(0)
        both(quarter - 1)
        g_arrive = share(gs[t], half_rows, 2 - t)
        loop(1, quarter - 1, both, 1)

        def arrive_all():
            k_arrive()
            g_arrive()

        return arrive_all

    n = tile // 2
    load.wait()
    loop(1, n - 1, lambda i: analyse_first(0, i))
    arrive()
    analyse_first(0, 0)
    analyse_first(0, n - 1)
    arrive = middle(0)
    shaped = xs[1][0]

    def keep(m):
        shaped[2 * m + 2], shaped[2 * m + 3] = make_first(0, m)

    loop(1, n - 1, keep)
    loop(2, n - 2, lambda i: analyse_first(1, i))
    arrive()
    keep(0)
    keep(n - 1)
    even, odd = make_first(0, -1)
    inside = jnp.where(has_down, 1.0, 0.0).astype(F32)
    shaped[0], shaped[1] = inside * even, inside * odd
    shaped[tile + 2] = jnp.where(has_up, 1.0, 0.0).astype(F32) * make_first(0, n, even_only=True)
    for i in (0, 1, n - 2, n - 1):
        analyse_first(1, i)
    arrive = middle(1)

    def put(m):
        out[2 * m], out[2 * m + 1] = make_first(1, m)

    loop(1, n - 1, put)
    arrive()
    put(0)
    put(n - 1)
    for sent in pending:
        sent()


def on_device(increment, filter_taps, band_roots, lats):
    lev, tile, lanes = increment.shape
    padded, side = -(-lev // 16) * 16, -(-lev // 128) * 128
    x = jnp.pad(jnp.transpose(increment, (1, 0, 2)), ((0, 0), (0, padded - lev), (0, 0)))
    def slabs(count):
        return pltpu.VMEM((count, padded, lanes), F32)

    counts = [tile >> (j + 1) for j in range(LEVELS)]
    scratch = [slabs(2 * n + 3) for n in counts[:2]] * 2
    scratch += [slabs(1)] * 4 + [slabs(7)] * 2 + [slabs(counts[1] + 2)] * 2
    scratch += [slabs(counts[0] + 4), slabs(counts[0] + 2)] * 2
    scratch += [slabs(counts[1] + 2), slabs(counts[0]), slabs(counts[0])]
    scratch += [pltpu.VMEM((8, padded, 2 * lanes), BF16)]
    copies = 2 + 2 * (2 + len(REACH) + 2 * 3)
    scratch += [
        pltpu.VMEM((FAR_T + 2, 2 * lanes, 2 * lanes), BF16),
        pltpu.VMEM((2 * (LEVELS + 1), 2 * padded, padded), BF16),
        pltpu.SMEM((filter_taps.size,), F32),
        pltpu.VMEM(band_roots.shape, F32),
        pltpu.VMEM((side, side), F32),
        pltpu.SemaphoreType.DMA((copies,)),
        pltpu.SemaphoreType.DMA((copies,)),
        pltpu.SemaphoreType.DMA,
        pltpu.SemaphoreType.DMA,
    ]
    y = pl.pallas_call(
        functools.partial(kernel, lats),
        out_shape=jax.ShapeDtypeStruct((tile, padded, lanes), F32),
        in_specs=[
            pl.BlockSpec(memory_space=pltpu.SMEM),
            pl.BlockSpec(memory_space=pl.ANY),
            pl.BlockSpec(memory_space=pl.ANY),
        ],
        out_specs=pl.BlockSpec(memory_space=pltpu.VMEM),
        scratch_shapes=scratch,
        compiler_params=pltpu.CompilerParams(
            collective_id=0, has_side_effects=True, vmem_limit_bytes=48 << 20
        ),
    )(filter_taps.reshape(-1), x, band_roots)
    return jnp.transpose(y[:, :lev], (1, 0, 2))


def solution(mesh):
    placed = (P("member", "lat", None), P(), P())
    return jax.shard_map(
        functools.partial(on_device, lats=mesh.shape["lat"]),
        mesh=mesh, in_specs=placed, out_specs=P("member", "lat", None), check_vma=False,
    )
```

```python
import functools
import math

import jax
import jax.numpy as jnp
from jax import lax
from jax.experimental import pallas as pl
from jax.experimental.pallas import tpu as pltpu
from jax.sharding import PartitionSpec as P

LEVELS = 4
NEAR, NEAR_T, FAR, FAR_T = 5, 8, 12, 17
REACH = (1, -1, 2, -2, 3, -3)
ROOT_TWO = math.sqrt(2.0)
F32, BF16 = jnp.float32, jnp.bfloat16


def halves_of(x):
    high = x.astype(BF16)
    return high, (x - high.astype(F32)).astype(BF16)


def dot(a, b):
    return jnp.dot(a, b, preferred_element_type=F32)


def kernel(lats, raw_taps, x_hbm, roots_hbm, out, *scratch):
    scratch = iter(scratch)

    def take(count):
        return [next(scratch) for _ in range(count)]

    xs = [take(2), take(2)]
    packs, lands = take(2), take(2)
    wides, seconds = take(2), take(2)
    gs, ks = take(2), take(2)
    g_second, part, hs, cats = take(4)
    wmats, mats, taps, roots, square, sends, recvs, load_sem, root_sem = scratch
    tile, lev, lanes = x_hbm.shape
    half = lanes // 2
    me = lax.axis_index("lat")
    has_down, has_up = me > 0, me < lats - 1
    mesh_ids = pl.DeviceIdType.MESH
    slots = iter(range(10_000))
    pending = []

    def tap(level, direction, kind, k):
        return taps[((level * 2 + direction) * 2 + kind) * 5 + k]

    def device(d):
        return {"lat": jnp.clip(me + d, 0, lats - 1)}

    def there(d):
        return me + d < lats if d > 0 else me + d >= 0

    def exchange(moves):
        waits = []
        for d, src, dst in moves:
            slot = next(slots)
            copy = pltpu.make_async_remote_copy(
                src_ref=src, dst_ref=dst, send_sem=sends.at[slot],
                recv_sem=recvs.at[slot], device_id=device(d), device_id_type=mesh_ids,
            )
            waits.append((d, copy))
            pl.when(there(d))(copy.start)
            pending.append(lambda d=d, copy=copy: pl.when(there(d))(copy.wait_send))

        def arrive():
            for d, copy in waits:
                pl.when(there(-d))(copy.wait_recv)

        return arrive

    load = pltpu.make_async_copy(x_hbm, xs[0][0].at[pl.ds(2, tile)], load_sem)
    load.start()
    fetch = pltpu.make_async_copy(roots_hbm, roots, root_sem)
    fetch.start()

    barrier = pltpu.get_barrier_semaphore()

    peers = 0
    for d in REACH:
        def greet(d=d):
            pl.semaphore_signal(barrier, inc=1, device_id=device(d), device_id_type=mesh_ids)

        pl.when(there(d))(greet)
        peers = peers + there(d).astype(jnp.int32)
    pl.semaphore_wait(barrier, peers)

    arrive = exchange([
        (1, x_hbm.at[pl.ds(tile - 2, 2)], xs[0][0].at[pl.ds(0, 2)]),
        (-1, x_hbm.at[pl.ds(0, 1)], xs[0][0].at[pl.ds(tile + 2, 1)]),
    ])

    for f in range(4 * LEVELS):
        values = [raw_taps[f * 5 + k].astype(F32) for k in range(5)]
        if f % 2:
            total = jnp.full((8, lanes), sum(v * v for v in values), F32)
            scale = (1.0 / jnp.sqrt(total))[0, 0]
        else:
            scale = (ROOT_TWO / jnp.full((8, lanes), sum(values), F32))[0, 0]
        for k in range(5):
            taps[f * 5 + k] = values[k] * (-scale if f % 2 and k % 2 else scale)

    def clear(ref, start, count):
        for r in range(count):
            ref[start + r] = jnp.zeros(ref.shape[1:], F32)

    half_rows, quarter = tile // 2, tile // 4
    edges_low, edges_high = [(xs[0][0], 0, 2)], [(xs[0][0], tile + 2, 1)]
    for t in range(2):
        rim = 2 - t
        edges_low += [(lands[t], 0, 1), (gs[t], 0, rim), (ks[t], 0, rim), (seconds[t], 0, 1)]
        edges_high += [(xs[t][1], half_rows + 2, 1), (gs[t], half_rows + rim, rim)]
        edges_high += [(ks[t], half_rows + rim, rim), (seconds[t], quarter + 1, 1)]

    @pl.when(jnp.logical_not(has_down))
    def _():
        for edge in edges_low:
            clear(*edge)

    @pl.when(jnp.logical_not(has_up))
    def _():
        for edge in edges_high:
            clear(*edge)

    for d in REACH:
        def blank(d=d):
            for t in range(2):
                clear(wides[t], 3 + d, 1)

        pl.when(jnp.logical_not(there(d)))(blank)
    cats[7] = jnp.zeros(cats.shape[1:], BF16)

    def keep_matrix(at, w):
        high, low = halves_of(w)
        wmats[at, pl.ds(0, lanes), pl.ds(0, lanes)] = high
        wmats[at, pl.ds(0, lanes), pl.ds(lanes, lanes)] = low
        wmats[at, pl.ds(lanes, lanes), pl.ds(0, lanes)] = high
        wmats[at, pl.ds(lanes, lanes), pl.ds(lanes, lanes)] = jnp.zeros_like(low)

    def build_wide(at, level, shift, flip):
        width = lanes >> level
        c = lax.broadcasted_iota(jnp.int32, (lanes, lanes), flip)
        o = lax.broadcasted_iota(jnp.int32, (lanes, lanes), 1 - flip)
        pitch = width if level == 2 else 4 * width
        row, col = c // pitch, c % pitch
        out_row, kind, out_col = o // (2 * width), (o // width) % 2, o % width
        is_low = out_col < width // 2
        t = col - 2 * jnp.where(is_low, out_col, out_col - width // 2) + 2
        u = row + shift - 2 * out_row + 2
        lon = jnp.zeros((lanes, lanes), F32)
        lat = jnp.zeros((lanes, lanes), F32)
        for k in range(5):
            lon = jnp.where(t == k, jnp.where(is_low, tap(level, 1, 0, k), tap(level, 1, 1, k)), lon)
            lat = jnp.where(u == k, jnp.where(kind == 0, tap(level, 0, 0, k), tap(level, 0, 1, k)), lat)
        keep_matrix(at, jnp.where(col < width, lon * lat, 0.0))

    def build_second():
        for q in (-1, 0, 1):
            build_wide(NEAR + q, 2, 4 * q, 0)
            build_wide(NEAR_T + q, 2, 4 * q, 1)

    def build_third():
        for q in range(-2, 4):
            build_wide(FAR + q, 3, 2 * q + 2, 0)
            if -2 < q < 2:
                build_wide(FAR_T + q, 3, 2 * q + 2, 1)

    for j in range(2):
        width = lanes >> j
        block = lanes if j == 0 else half
        for flip in range(2):
            c = lax.broadcasted_iota(jnp.int32, (lanes, lanes), flip)
            o = lax.broadcasted_iota(jnp.int32, (lanes, lanes), 1 - flip)
            same = True
            if j:
                same = (c < half) == (o < half)
                c = jnp.where(c < half, c, c - half)
                o = jnp.where(o < half, o, o - half)
            is_low = o < width // 2
            t = c - 2 * jnp.where(is_low, o, o - width // 2) + 2
            w = jnp.zeros((lanes, lanes), F32)
            for k in range(5):
                w = jnp.where(t == k, jnp.where(is_low, tap(j, 1, 0, k), tap(j, 1, 1, k)), w)
            w = jnp.where((c < width) & (o < width) & same, w, 0.0)
            keep_matrix(2 * j + flip, w)
    fetch.wait()
    square[...] = jnp.zeros(square.shape, F32)
    count = roots.shape[1]

    def split_roots(t):
        for b in range(LEVELS + 1):
            square[pl.ds(0, count), pl.ds(0, count)] = roots[b]
            m = square[...].T if t else square[...]
            high, low = halves_of(m[:lev, :lev])
            mats[t * (LEVELS + 1) + b, pl.ds(0, lev)] = high
            mats[t * (LEVELS + 1) + b, pl.ds(lev, lev)] = low

    split_roots(0)

    def along_lon(x, at):
        high, low = halves_of(x)
        r = dot(jnp.concatenate([high, low], axis=1), wmats[at])
        return r[:, :lanes] + r[:, lanes:]

    def vertical(x, t, band):
        b = t * (LEVELS + 1) + band
        high, low = halves_of(x)
        r = dot(mats[b], high)
        return r[:lev] + r[lev:] + dot(mats[b, pl.ds(0, lev)], low)

    def loop(start, stop, body, step=3):
        count = max(stop - start, 0)
        whole = count // step
        if whole > 1:
            def several(i, _):
                for s in range(step):
                    body(start + i * step + s)
                return 0

            lax.fori_loop(0, whole, several, 0)
        else:
            whole = 0
        for i in range(start + whole * step, stop):
            body(i)

    lane = lax.broadcasted_iota(jnp.int32, (lev, lanes), 1)
    lane8 = lax.broadcasted_iota(jnp.int32, (8, lanes), 1)

    def swap(x):
        return pltpu.roll(x, half, 1)

    def twice(x):
        return jnp.where(lane < half, x, swap(x))

    def weighted(level, pairs):
        total = None
        for k, x in pairs:
            scale = jnp.where(lane8 < half, tap(level, 0, 0, k), tap(level, 0, 1, k))
            term = scale[None] * x.reshape(lev // 8, 8, lanes)
            total = term if total is None else total + term
        return total.reshape(lev, lanes)

    def analyse_first(t, i):
        rows = [xs[t][0][2 * i + k] for k in range(5)]
        low = sum(tap(0, 0, 0, k) * rows[k] for k in range(5))
        high = sum(tap(0, 0, 1, k) * rows[k] for k in range(5))
        both = along_lon(jnp.concatenate([low, high], axis=0), 0)
        part[i] = both[:lev]
        hs[i] = both[lev:]
        xs[t][1][i + 2] = twice(both[:lev])

    def analyse(t, i):
        rows = [(k, xs[t][1][2 * i + k]) for k in range(5)]
        seconds[t][i + 1] = along_lon(weighted(1, rows), 2)

    def share_coarse(t):
        rows, pack, land = xs[t][1], packs[t], lands[t]
        pack[0] = jnp.where(lane < half, rows[half_rows], rows[half_rows + 1])
        wait = exchange([
            (1, pack, land),
            (-1, rows.at[pl.ds(2, 1)], rows.at[pl.ds(half_rows + 2, 1)]),
        ])

        def arrived():
            wait()
            got = land[0]
            turned = swap(got)
            rows[0] = jnp.where(lane < half, got, turned)
            rows[1] = jnp.where(lane < half, turned, got)

        return arrived

    def share(ref, n, rim):
        return exchange([
            (1, ref.at[pl.ds(n, rim)], ref.at[pl.ds(0, rim)]),
            (-1, ref.at[pl.ds(rim, rim)], ref.at[pl.ds(n + rim, rim)]),
        ])

    def weigh_first(t, i):
        pair = vertical(jnp.concatenate([part[i], hs[i]], axis=1), t, 0)
        part[i] = pair[:, :lanes]
        ks[t][i + 2 - t] = along_lon(pair[:, lanes:], 1)

    def weigh_second(t):
        for i in range(0, quarter, 2):
            pair = [seconds[t][i + s + 1] for s in range(2)]
            pair = vertical(jnp.concatenate(pair, axis=1), t, 1)
            for s in range(2):
                seconds[t][i + s + 1] = pair[:, s * lanes:(s + 1) * lanes]

    def lift_second(t, i, coarse):
        chosen = jnp.where(lane < lanes // 4, coarse, seconds[t][i + 1])
        return along_lon(chosen, 3)

    def lift_first(t, i, coarse):
        chosen = jnp.where(lane < half, coarse, part[i])
        gs[t][i + 2 - t] = along_lon(chosen, 1)

    def make(m):
        g = [g_second[m + s] for s in range(3)]
        even = weighted(1, [(4 - 2 * s, g[s]) for s in range(3)])
        odd = weighted(1, [(5 - 2 * s, g[s]) for s in (1, 2)])
        return even + swap(even), odd + swap(odd)

    def make_first(t, m, even_only=False):
        rim = 2 - t
        g = [gs[t][m + rim + s] for s in (-1, 0, 1)]
        k = [ks[t][m + rim + s] for s in (-1, 0, 1)]
        even = sum(tap(0, 0, 0, 4 - 2 * s) * g[s] + tap(0, 0, 1, 4 - 2 * s) * k[s] for s in range(3))
        if even_only:
            return even
        odd = sum(tap(0, 0, 0, 5 - 2 * s) * g[s] + tap(0, 0, 1, 5 - 2 * s) * k[s] for s in (1, 2))
        return even, odd

    def joined(x):
        return jnp.concatenate(halves_of(x), axis=1)

    def folded(r):
        return r[:, :lanes] + r[:, lanes:]

    def present(s):
        return jnp.where((me + s >= 0) & (me + s < lats), 1.0, 0.0).astype(F32)

    def cat_rows(start, count):
        return cats[pl.ds(start, count)].reshape(count * lev, 2 * lanes)

    def deep(t, near_arrive, far_arrive):
        def coarsen(start, count):
            q = dot(cat_rows(start, count), wmats[NEAR])
            q = q + dot(cat_rows(start - 1, count), wmats[NEAR - 1])
            q = folded(q + dot(cat_rows(start + 1, count), wmats[NEAR + 1]))
            return [present(start + s - 3) * q[s * lev:(s + 1) * lev] for s in range(count)]

        near_arrive()
        for s in range(1, 6):
            cats[s] = joined(wides[t][s])
        middle_q = coarsen(2, 3)
        second = vertical(jnp.concatenate(middle_q, axis=1), t, 2)
        partial = sum(dot(joined(middle_q[s]), wmats[FAR + s - 1]) for s in range(3))
        far_arrive()
        for s in (0, 6):
            cats[s] = joined(wides[t][s])
        q = coarsen(1, 1) + middle_q + coarsen(5, 2)
        third = folded(partial + sum(dot(joined(q[s]), wmats[FAR + s - 2]) for s in (0, 4, 5)))
        owner = me + lane // (lanes // 4) - 1
        third = jnp.where((owner >= 0) & (owner < lats), third, 0.0)
        top = vertical(third, t, LEVELS)
        third = jnp.where(lane % (lanes // 4) < lanes // 16, top, vertical(third, t, 3))
        third = joined(third)
        lifted = []
        for s in (-1, 0, 1):
            c = folded(dot(third, wmats[FAR_T + s]))
            d = second[:, (s + 1) * lanes:(s + 2) * lanes]
            lifted.append(joined(present(s) * jnp.where(lane % half < lanes // 8, c, d)))

        def spread(pairs):
            return folded(sum(dot(lifted[s + 1], wmats[NEAR_T + d]) for s, d in pairs))

        return (
            spread(((-1, 0), (0, -1))),
            spread(((-1, 1), (0, 0), (1, -1))),
            spread(((0, 1), (1, 0))),
        )

    def middle(t):
        arrived = share_coarse(t)
        if t == 0:
            build_second()
        loop(0, half_rows, lambda i: weigh_first(t, i), 4)
        loop(1, quarter - 1, lambda i: analyse(t, i))
        arrived()
        analyse(t, 0)
        analyse(t, quarter - 1)
        own = seconds[t][1]
        for r in range(1, quarter):
            turned = pltpu.roll(seconds[t][r + 1], r * (lanes // 4), 1)
            own = jnp.where(lane < r * (lanes // 4), own, turned)
        wide = wides[t]
        wide[3] = own
        moves = [(d, wide.at[pl.ds(3, 1)], wide.at[pl.ds(3 - d, 1)]) for d in REACH]
        near_arrive, far_arrive = exchange(moves[:4]), exchange(moves[4:])
        weigh_second(t)
        second_arrive = share(seconds[t], quarter, 1)
        if t == 0:
            build_third()
            split_roots(1)
        before, own, after = deep(t, near_arrive, far_arrive)
        k_arrive = share(ks[t], half_rows, 2 - t)
        for r in range(quarter):
            coarse = own if r == 0 else pltpu.roll(own, lanes - r * (lanes // 4), 1)
            g_second[r + 1] = lift_second(t, r, coarse)

        def both(m):
            even, odd = make(m)
            lift_first(t, 2 * m, even)
            lift_first(t, 2 * m + 1, odd)

        second_arrive()
        before = pltpu.roll(before, lanes // 4, 1)
        g_second[0] = present(-1) * lift_second(t, -1, before)
        g_second[quarter + 1] = present(1) * lift_second(t, quarter, after)
        both(0)
        both(quarter - 1)
        g_arrive = share(gs[t], half_rows, 2 - t)
        loop(1, quarter - 1, both, 1)

        def arrive_all():
            k_arrive()
            g_arrive()

        return arrive_all

    n = tile // 2
    load.wait()
    loop(1, n - 1, lambda i: analyse_first(0, i))
    arrive()
    analyse_first(0, 0)
    analyse_first(0, n - 1)
    arrive = middle(0)
    shaped = xs[1][0]

    def keep(m):
        shaped[2 * m + 2], shaped[2 * m + 3] = make_first(0, m)

    loop(1, n - 1, keep)
    loop(2, n - 2, lambda i: analyse_first(1, i))
    arrive()
    keep(0)
    keep(n - 1)
    even, odd = make_first(0, -1)
    inside = jnp.where(has_down, 1.0, 0.0).astype(F32)
    shaped[0], shaped[1] = inside * even, inside * odd
    shaped[tile + 2] = jnp.where(has_up, 1.0, 0.0).astype(F32) * make_first(0, n, even_only=True)
    for i in (0, 1, n - 2, n - 1):
        analyse_first(1, i)
    arrive = middle(1)

    def put(m):
        out[2 * m], out[2 * m + 1] = make_first(1, m)

    loop(1, n - 1, put)
    arrive()
    put(0)
    put(n - 1)
    for sent in pending:
        sent()


def on_device(increment, filter_taps, band_roots, lats):
    lev, tile, lanes = increment.shape
    padded, side = -(-lev // 16) * 16, -(-lev // 128) * 128
    x = jnp.pad(jnp.transpose(increment, (1, 0, 2)), ((0, 0), (0, padded - lev), (0, 0)))
    def slabs(count):
        return pltpu.VMEM((count, padded, lanes), F32)

    counts = [tile >> (j + 1) for j in range(LEVELS)]
    scratch = [slabs(2 * n + 3) for n in counts[:2]] * 2
    scratch += [slabs(1)] * 4 + [slabs(7)] * 2 + [slabs(counts[1] + 2)] * 2
    scratch += [slabs(counts[0] + 4), slabs(counts[0] + 2)] * 2
    scratch += [slabs(counts[1] + 2), slabs(counts[0]), slabs(counts[0])]
    scratch += [pltpu.VMEM((8, padded, 2 * lanes), BF16)]
    copies = 2 + 2 * (2 + len(REACH) + 2 * 3)
    scratch += [
        pltpu.VMEM((FAR_T + 2, 2 * lanes, 2 * lanes), BF16),
        pltpu.VMEM((2 * (LEVELS + 1), 2 * padded, padded), BF16),
        pltpu.SMEM((filter_taps.size,), F32),
        pltpu.VMEM(band_roots.shape, F32),
        pltpu.VMEM((side, side), F32),
        pltpu.SemaphoreType.DMA((copies,)),
        pltpu.SemaphoreType.DMA((copies,)),
        pltpu.SemaphoreType.DMA,
        pltpu.SemaphoreType.DMA,
    ]
    y = pl.pallas_call(
        functools.partial(kernel, lats),
        out_shape=jax.ShapeDtypeStruct((tile, padded, lanes), F32),
        in_specs=[
            pl.BlockSpec(memory_space=pltpu.SMEM),
            pl.BlockSpec(memory_space=pl.ANY),
            pl.BlockSpec(memory_space=pl.ANY),
        ],
        out_specs=pl.BlockSpec(memory_space=pltpu.VMEM),
        scratch_shapes=scratch,
        compiler_params=pltpu.CompilerParams(
            collective_id=0, has_side_effects=True, vmem_limit_bytes=48 << 20
        ),
    )(filter_taps.reshape(-1), x, band_roots)
    return jnp.transpose(y[:, :lev], (1, 0, 2))


def solution(mesh):
    placed = (P("member", "lat", None), P(), P())
    return jax.shard_map(
        functools.partial(on_device, lats=mesh.shape["lat"]),
        mesh=mesh, in_specs=placed, out_specs=P("member", "lat", None), check_vma=False,
    )
```
